256 devices in a mesh: replica: 32 (over y, z_lo, core), fsdp: 8 (over x, z_hi).
Axes of the slice: x: 4, y: 4, z: 8 (z_hi: 2, z_lo: 4; z = z_hi * 4 + z_lo), core: 2. Of those that a mesh axis runs over, the one named last changes fastest.
Arguments:
- tokens: bfloat16 [98304, 8192], P(('replica', 'fsdp')), may hold values from -6 to 6
- inner_weight: bfloat16 [32, 8192, 512], P('replica', 'fsdp'), may hold values from -0.0625 to 0.0625
- cotangent: bfloat16 [98304, 512], P(('replica', 'fsdp')), may hold values from -0.059814453 to 0.059814453
- local_weights: bfloat16 [32, 2, 8192, 896], P('replica', None, 'fsdp'), may hold values from -3 to 3
- anchor: bfloat16 [2, 8, 1024, 896], P(None, 'fsdp', 'replica'), may hold values from -1.5 to 1.5
- momentum: float32 [2, 8, 1024, 896], P(None, 'fsdp', 'replica'), may hold values from -1.5 to 1.5
Outputs:
- keys: bfloat16 [98304, 512], P(('replica', 'fsdp'))
- weight_grad: bfloat16 [32, 8192, 512], P('replica', 'fsdp')
- new_weights: bfloat16 [2, 8192, 896], P(None, 'fsdp')
- new_momentum: float32 [2, 8, 1024, 896], P(None, 'fsdp', 'replica')
The draws below stay inside these ranges and needn't reach their ends.
All inputs are finite; a program needn't handle non-finite values.
Results may differ from the reference program's by a relative error of at most 0.017.
Values may be sent and summed in bfloat16 or wider, within the bound.
A program may use at most 128 MiB of HBM per device.

```python
import jax
import jax.numpy as jnp
from jax import lax

D = 8192
KV = 896
KW = 512
TOK_DEV = 384
TOKENS = 98304
N_REPLICA = 32
N_FSDP = 8


def raised(result, rng, source, target, parts, factor):
    def block_of(dim):
        return (jnp.arange(result.shape[dim]) // (result.shape[dim] // parts)).reshape((-1,) + (1,) * (result.ndim - 1 - dim))

    one_side = jax.random.permutation(rng, parts)[block_of(target)]
    other_side = (block_of(target) + parts // 2) % parts
    return jnp.where((block_of(source) == one_side) | (block_of(source) == other_side), factor * result, result)


def levels(key, shape, split, smallest, largest):
    gain = 1.0
    for position, blocks in split:
        draws = jax.random.uniform(jax.random.fold_in(jax.random.fold_in(key, 6), position), (blocks,), jnp.float32, smallest / len(split), largest / len(split))
        gain = gain * jnp.repeat(jnp.exp(draws), shape[position] // blocks).reshape((-1,) + (1,) * (len(shape) - 1 - position))
    return gain


def noise(own_key, dims, deviation, reach, pieces=(), held_as=jnp.bfloat16):
    result = jax.random.normal(own_key, dims, jnp.float32) * deviation
    if len(pieces) > 0:
        result = levels(own_key, dims, pieces, -0.22, 0.18) * result
    return jnp.clip(result, min=-reach, max=reach).astype(held_as)


def gaussian_with(key, extent, deviation, reach, pieces, heavy, kind=jnp.bfloat16):
    values = deviation * jax.random.normal(key, extent, jnp.float32)
    if pieces:
        values = values * levels(key, extent, pieces, -0.22, 0.18)
    return jnp.clip(raised(values, jax.random.fold_in(key, 3), *heavy), -reach, reach).astype(kind)


def setup_inputs(seed: int = 0) -> dict:
    streams_of = jax.random.split(jax.random.key(seed), 7)
    return {
        "tokens": noise(streams_of[0], (TOKENS, D), 1.0, 6.0, ((0, 256),)),
        "inner_weight": noise(streams_of[1], (N_REPLICA, D, KW), D ** -0.5, 0.0625, ((0, 32), (1, 8))),
        "cotangent": noise(streams_of[2], (TOKENS, KW), 0.01, 0.059814453, ((0, 256),)),
        "local_weights": gaussian_with(streams_of[3], (N_REPLICA, 2, D, KV), 0.5, 3.0, ((0, 32), (2, 8)), (0, 2, 32, 2.75)),
        "anchor": noise(streams_of[4], (2, N_FSDP, D // N_FSDP, KV), 0.25, 1.5, ((1, 8), (2, 32))),
        "momentum": noise(streams_of[5], (2, N_FSDP, D // N_FSDP, KV), 0.25, 1.5, ((1, 8), (2, 32)), jnp.float32),
    }


outer_rate = 0.7
momentum_decay = 0.9


def reference(tokens, inner_weight, cotangent, local_weights, anchor, momentum):
    def accumulate(running, replica_slab):
        return running + replica_slab.astype(jnp.float32), None

    summed, unused = lax.scan(accumulate, jnp.zeros((2, D, KV), jnp.float32), local_weights)
    average = (summed / N_REPLICA).reshape(2, N_FSDP, D // N_FSDP, KV)
    anchor_now = anchor.astype(jnp.float32)
    pseudo_grad = anchor_now - average
    momentum_new = momentum_decay * momentum + pseudo_grad
    new_anchor = (anchor_now - outer_rate * (pseudo_grad + momentum_decay * momentum_new)).astype(jnp.bfloat16)
    new_weights = new_anchor.reshape(2, D, KV)

    token_sets = tokens.reshape(N_REPLICA, N_FSDP, TOK_DEV, D)
    cot_sets = cotangent.reshape(N_REPLICA, N_FSDP, TOK_DEV, KW)

    def one_replica(packed):
        token_set, cot_set, weight = packed
        key_rows = jnp.dot(token_set.reshape(N_FSDP * TOK_DEV, D), weight,
                           preferred_element_type=jnp.float32).astype(jnp.bfloat16)
        block_terms = jnp.einsum("btd,btk->bdk", token_set.astype(jnp.float32),
                                 cot_set.astype(jnp.float32)).astype(jnp.bfloat16)
        grad_sum = jnp.sum(block_terms.astype(jnp.float32), axis=0).astype(jnp.bfloat16)
        return key_rows, grad_sum

    key_all, weight_grad = lax.map(one_replica, (token_sets, cot_sets, inner_weight))
    keys = key_all.reshape(TOKENS, KW)
    return keys, weight_grad, new_weights, momentum_new
```

```python
import jax
import jax.numpy as jnp
from jax import lax
from jax.experimental import pallas as pl
from jax.experimental.pallas import tpu as pltpu
from jax.sharding import PartitionSpec as P

outer_rate = 0.7
momentum_decay = 0.9
MESH = pl.DeviceIdType.MESH
F32 = jnp.float32
BF16 = jnp.bfloat16

X, Y, ZL = 4, 4, 4
TOK, SLAB, KW = 384, 1024, 512
ROWS, KV = 32, 896
WCH = 4
GCH = 4
LAST_W = 1

L_, W_, C_, TO, TN, YR, ZR, ZG, YG, CG, G_, K_ = (0, 2, 6, 9, 12, 15, 18, 21, 24, 27, 28, 32)
NSEM = 35


def kernel(tok, wgt, cot, loc, anc, mom, keys, wgrad, neww, newm,
           tbuf, cbuf, wbuf, lown, lrecv, s1, s1r, s2, s2f, s2r, ancv, momv, piece, momo,
           kacc, ksend, krecv, kout, gsend, grecv, gown, gout, ss, rs, ls, os):
    r = lax.axis_index("replica")
    f = lax.axis_index("fsdp")
    y, zl, c = r // 8, (r // 2) % 4, r % 2
    x, zh = f // 2, f % 2

    def at_x(k):
        return (r, lax.rem(x + k, X) * 2 + zh)

    def at_y(k):
        return (lax.rem(y + k, Y) * 8 + zl * 2 + c, f)

    def at_z(k):
        return (y * 8 + lax.rem(zl + k, ZL) * 2 + c, f)

    across = (r, x * 2 + (1 - zh))
    sibling = (y * 8 + zl * 2 + (1 - c), f)

    barrier = pltpu.get_barrier_semaphore()
    peers = [across, sibling]
    for k in (1, 2, 3):
        peers += [at_x(k), at_y(k), at_z(k)]
    for p in peers:
        pl.semaphore_signal(barrier, inc=1, device_id=p, device_id_type=MESH)

    def load(i, src, dst):
        cp = pltpu.make_async_copy(src, dst, ls.at[i])
        cp.start()
        return cp

    def column(who, half):
        return pl.ds(pl.multiple_of((who * 2 + half) * SLAB, SLAB), SLAB)

    ld_l = [load(m, loc.at[m, :, :, c], lown.at[m]) for m in range(2)]
    ld_a = load(2, anc, ancv)
    ld_m = load(3, mom, momv)
    ld_c = load(4, cot, cbuf.at[pl.ds(0, TOK)])
    ld_to = load(5, tok.at[:, column(x, 1 - zh)], tbuf.at[0, pl.ds(0, TOK)])
    ld_tn = load(6, tok.at[:, column(x, zh)], tbuf.at[1, pl.ds(0, TOK)])
    ld_w = load(7, wgt, wbuf.at[1])

    pl.semaphore_wait(barrier, len(peers))

    def send(i, src, dst, to):
        cp = pltpu.make_async_remote_copy(
            src_ref=src, dst_ref=dst, send_sem=ss.at[i], recv_sem=rs.at[i],
            device_id=to, device_id_type=MESH)
        cp.start()
        return cp

    def send_w(j):
        rows = pl.ds(j * (SLAB // WCH), SLAB // WCH)
        return send(W_ + j, wgt.at[rows], wbuf.at[0, rows], across)

    c_l = [send(L_ + m, loc.at[m, :, :, 1 - c], lrecv.at[m], sibling) for m in range(2)]
    c_w = [send_w(j) for j in range(WCH - LAST_W)]
    c_c = [send(C_ + k - 1, cot, cbuf.at[pl.ds(k * TOK, TOK)], at_x(k)) for k in (1, 3, 2)]
    c_to = [send(TO + k - 1, tok.at[:, column(lax.rem(x + k, X), 1 - zh)],
                 tbuf.at[0, pl.ds(k * TOK, TOK)], at_x(k)) for k in (1, 3, 2)]
    c_tn = [send(TN + k - 1, tok.at[:, column(lax.rem(x + k, X), zh)],
                 tbuf.at[1, pl.ds(k * TOK, TOK)], at_x(k)) for k in (1, 3, 2)]

    for m in range(2):
        ld_l[m].wait()
        c_l[m].wait_recv()

        @pl.loop(0, Y * ZL)
        def _(i):
            a, b = i // ZL, i % ZL
            s1[m, a, b] = (lown[m, a, b].astype(F32) + lrecv[m, a, b].astype(F32)).astype(BF16)

    c_y = [send(YR + k - 1, s1.at[:, lax.rem(y + k, Y)], s1r.at[k - 1], at_y(k)) for k in (1, 3, 2)]
    for cp in c_y:
        cp.wait_recv()

    @pl.loop(0, 2 * ZL)
    def _(i):
        m, b = i // ZL, i % ZL
        total = lown[m, y, b].astype(F32) + lrecv[m, y, b].astype(F32)
        for k in range(3):
            total += s1r[k, m, b].astype(F32)
        s2f[m, b] = total
        s2[m, b] = total.astype(BF16)

    c_z = [send(ZR + k - 1, s2.at[:, lax.rem(zl + k, ZL)], s2r.at[k - 1], at_z(k)) for k in (1, 3, 2)]
    c_w += [send_w(j) for j in range(WCH - LAST_W, WCH)]
    ld_a.wait()
    ld_m.wait()
    for cp in c_z:
        cp.wait_recv()

    @pl.loop(0, 2)
    def _(m):
        total = s2f[m, zl]
        for k in range(3):
            total += s2r[k, m].astype(F32)
        anchor_now = ancv[m].astype(F32)
        pseudo = anchor_now - total / 32.0
        momentum_new = momentum_decay * momv[m] + pseudo
        momo[m] = momentum_new
        piece[m] = (anchor_now - outer_rate * (pseudo + momentum_decay * momentum_new)).astype(BF16)

    def store(i, src, dst):
        cp = pltpu.make_async_copy(src, dst, os.at[i])
        cp.start()
        return cp

    c_zg = [send(ZG + k - 1, piece, neww.at[:, y, zl, c], at_z(k)) for k in (1, 3, 2)]
    st_p = store(0, piece, neww.at[:, y, zl, c])
    st_m = store(1, momo, newm)

    ld_c.wait()
    ld_to.wait()
    for cp in c_c + c_to:
        cp.wait_recv()
    gw = SLAB // GCH

    def grad(half, j):
        return lax.dot_general(
            tbuf[half, :, pl.ds(j * gw, gw)], cbuf[...],
            (((0,), (0,)), ((), ())), preferred_element_type=F32)

    c_g = []
    for j in range(GCH):
        rows = pl.ds(j * gw, gw)
        gsend[rows] = grad(0, j).astype(BF16)
        c_g.append(send(G_ + j, gsend.at[rows], grecv.at[rows], across))

    st_p.wait()
    for cp in c_zg:
        cp.wait_recv()
    mine = neww.at[:, y, :, c]
    c_yg = [send(YG + k - 1, mine, mine, at_y(k)) for k in (1, 3, 2)]

    for cp in c_w:
        cp.wait_recv()

    @pl.loop(0, X)
    def _(k):
        rows = pl.ds(pl.multiple_of(k * TOK, TOK), TOK)
        kacc[rows] = jnp.dot(tbuf[0, rows], wbuf[0], preferred_element_type=F32)

    ld_w.wait()
    ld_tn.wait()
    for cp in c_tn:
        cp.wait_recv()
    c_k = []
    for k in (1, 3, 2, 0):
        rows = pl.ds(k * TOK, TOK)
        part = kacc[rows] + jnp.dot(tbuf[1, rows], wbuf[1], preferred_element_type=F32)
        if k:
            ksend[k - 1] = part.astype(BF16)
            c_k.append(send(K_ + k - 1, ksend.at[k - 1], krecv.at[k - 1], at_x(X - k)))
        else:
            kacc[rows] = part

    for cp in c_yg:
        cp.wait_recv()
    c_cg = send(CG, neww.at[:, :, :, c], neww.at[:, :, :, c], sibling)

    for j in range(GCH):
        gown[pl.ds(j * gw, gw)] = grad(1, j)

    for cp in c_k:
        cp.wait_recv()

    @pl.loop(0, 4)
    def _(i):
        rows = pl.ds(pl.multiple_of(i * (TOK // 4), TOK // 4), TOK // 4)
        total = kacc[rows]
        for k in range(3):
            total += krecv[k, rows].astype(F32)
        kout[rows] = total.astype(BF16)

    st_k = store(2, kout, keys)
    st_g = []
    for j in range(GCH):
        c_g[j].wait_recv()
        rows = pl.ds(j * gw, gw)
        gout[rows] = (gown[rows] + grecv[rows].astype(F32)).astype(BF16)
        st_g.append(store(3 + j, gout.at[rows], wgrad.at[rows]))
    c_cg.wait_recv()
    for cp in c_l + c_w + c_c + c_to + c_tn + c_y + c_z + c_zg + c_yg + [c_cg] + c_g + c_k:
        cp.wait_send()
    for cp in [st_m, st_k] + st_g:
        cp.wait()


def shards(tokens, inner_weight, cotangent, local_weights, anchor, momentum):
    any_space = pl.BlockSpec(memory_space=pl.ANY)
    vm = pltpu.VMEM
    keys, wgrad, neww, newm = pl.pallas_call(
        kernel,
        name="diloco_step",
        out_shape=(
            jax.ShapeDtypeStruct((TOK, KW), BF16),
            jax.ShapeDtypeStruct((SLAB, KW), BF16),
            jax.ShapeDtypeStruct((2, Y, ZL, 2, ROWS, KV), BF16),
            jax.ShapeDtypeStruct((2, ROWS, KV), F32),
        ),
        in_specs=[any_space] * 6,
        out_specs=[any_space] * 4,
        scratch_shapes=[
            vm((2, X * TOK, SLAB), BF16), vm((X * TOK, KW), BF16), vm((2, SLAB, KW), BF16),
            vm((2, Y, ZL, ROWS, KV), BF16), vm((2, Y, ZL, ROWS, KV), BF16),
            vm((2, Y, ZL, ROWS, KV), BF16), vm((3, 2, ZL, ROWS, KV), BF16),
            vm((2, ZL, ROWS, KV), BF16), vm((2, ZL, ROWS, KV), F32), vm((3, 2, ROWS, KV), BF16),
            vm((2, ROWS, KV), BF16), vm((2, ROWS, KV), F32),
            vm((2, ROWS, KV), BF16), vm((2, ROWS, KV), F32),
            vm((X * TOK, KW), F32), vm((3, TOK, KW), BF16), vm((3, TOK, KW), BF16), vm((TOK, KW), BF16),
            vm((SLAB, KW), BF16), vm((SLAB, KW), BF16), vm((SLAB, KW), F32), vm((SLAB, KW), BF16),
            pltpu.SemaphoreType.DMA((NSEM,)), pltpu.SemaphoreType.DMA((NSEM,)),
            pltpu.SemaphoreType.DMA((8,)), pltpu.SemaphoreType.DMA((3 + GCH,)),
        ],
        compiler_params=pltpu.CompilerParams(collective_id=0, has_side_effects=True),
    )(
        tokens,
        inner_weight[0],
        cotangent,
        local_weights.reshape(2, Y, ZL, 2, ROWS, KV),
        anchor.reshape(2, ROWS, KV),
        momentum.reshape(2, ROWS, KV),
    )
    return (
        keys,
        wgrad[None],
        neww.reshape(2, Y * ZL * 2 * ROWS, KV),
        newm[:, None],
    )


def solution(mesh):
    return jax.shard_map(
        shards,
        mesh=mesh,
        in_specs=(
            P(("replica", "fsdp"), None),
            P("replica", "fsdp", None),
            P(("replica", "fsdp"), None),
            P("replica", None, "fsdp", None),
            P(None, "fsdp", "replica", None),
            P(None, "fsdp", "replica", None),
        ),
        out_specs=(
            P(("replica", "fsdp"), None),
            P("replica", "fsdp", None),
            P(None, "fsdp", None),
            P(None, "fsdp", "replica", None),
        ),
        check_vma=False,
    )
```

```python
import jax
import jax.numpy as jnp
from jax import lax
from jax.experimental import pallas as pl
from jax.experimental.pallas import tpu as pltpu
from jax.sharding import PartitionSpec as P

outer_rate = 0.7
momentum_decay = 0.9
MESH = pl.DeviceIdType.MESH
F32 = jnp.float32
BF16 = jnp.bfloat16

X, Y, ZL = 4, 4, 4
TOK, SLAB, KW = 384, 1024, 512
ROWS, KV = 32, 896
WCH = 4
GCH = 4
LAST_W = 1

L_, W_, C_, TO, TN, YR, ZR, ZG, YG, CG, G_, K_ = (0, 2, 6, 9, 12, 15, 18, 21, 24, 27, 28, 32)
F_, V_ = 35, 39
NSEM = 43


def kernel(tok, wgt, cot, loc, anc, mom, keys, wgrad, neww, newm,
           tbuf, cbuf, wbuf, lown, lrecv, s1, s1r, s2, s2f, s2r, ancv, momv, piece, momo,
           kacc, ksend, krecv, kout, gsend, grecv, gown, gout, hop, ss, rs, ls, os):
    r = lax.axis_index("replica")
    f = lax.axis_index("fsdp")
    y, zl, c = r // 8, (r // 2) % 4, r % 2
    x, zh = f // 2, f % 2

    def at_x(k):
        return (r, lax.rem(x + k, X) * 2 + zh)

    def at_y(k):
        return (lax.rem(y + k, Y) * 8 + zl * 2 + c, f)

    def at_z(k):
        return (y * 8 + lax.rem(zl + k, ZL) * 2 + c, f)

    across = (r, x * 2 + (1 - zh))

    def ring_z(k):
        z = lax.rem(zh * ZL + zl + k, 2 * ZL)
        return (y * 8 + lax.rem(z, ZL) * 2 + c, x * 2 + z // ZL)

    def relay_to(j):
        return ring_z(5 if j % 2 else 3)

    def relay_on(j):
        return ring_z(7 if j % 2 else 1)

    sibling = (y * 8 + zl * 2 + (1 - c), f)

    barrier = pltpu.get_barrier_semaphore()
    peers = [across, sibling]
    for k in (1, 2, 3):
        peers += [at_x(k), at_y(k), at_z(k)]
    peers += [ring_z(k) for k in (1, 3, 5, 7)]
    for p in peers:
        pl.semaphore_signal(barrier, inc=1, device_id=p, device_id_type=MESH)

    def load(i, src, dst):
        cp = pltpu.make_async_copy(src, dst, ls.at[i])
        cp.start()
        return cp

    def column(who, half):
        return pl.ds(pl.multiple_of((who * 2 + half) * SLAB, SLAB), SLAB)

    ld_l = [load(m, loc.at[m, :, :, c], lown.at[m]) for m in range(2)]
    ld_a = load(2, anc, ancv)
    ld_m = load(3, mom, momv)
    ld_c = load(4, cot, cbuf.at[pl.ds(0, TOK)])
    ld_to = load(5, tok.at[:, column(x, 1 - zh)], tbuf.at[0, pl.ds(0, TOK)])
    ld_tn = load(6, tok.at[:, column(x, zh)], tbuf.at[1, pl.ds(0, TOK)])
    ld_w = load(7, wgt, wbuf.at[1])

    pl.semaphore_wait(barrier, len(peers))

    def send(i, src, dst, to):
        cp = pltpu.make_async_remote_copy(
            src_ref=src, dst_ref=dst, send_sem=ss.at[i], recv_sem=rs.at[i],
            device_id=to, device_id_type=MESH)
        cp.start()
        return cp

    def send_w(j):
        rows = pl.ds(j * (SLAB // WCH), SLAB // WCH)
        return send(W_ + j, wgt.at[rows], wbuf.at[0, rows], across)

    c_l = [send(L_ + m, loc.at[m, :, :, 1 - c], lrecv.at[m], sibling) for m in range(2)]
    c_w = [send_w(j) for j in range(WCH - LAST_W)]
    c_c = [send(C_ + k - 1, cot, cbuf.at[pl.ds(k * TOK, TOK)], at_x(k)) for k in (1, 3, 2)]
    c_to = [send(TO + k - 1, tok.at[:, column(lax.rem(x + k, X), 1 - zh)],
                 tbuf.at[0, pl.ds(k * TOK, TOK)], at_x(k)) for k in (1, 3, 2)]
    c_tn = [send(TN + k - 1, tok.at[:, column(lax.rem(x + k, X), zh)],
                 tbuf.at[1, pl.ds(k * TOK, TOK)], at_x(k)) for k in (1, 3, 2)]

    for m in range(2):
        ld_l[m].wait()
        c_l[m].wait_recv()

        @pl.loop(0, Y * ZL)
        def _(i):
            a, b = i // ZL, i % ZL
            s1[m, a, b] = (lown[m, a, b].astype(F32) + lrecv[m, a, b].astype(F32)).astype(BF16)

    c_y = [send(YR + k - 1, s1.at[:, lax.rem(y + k, Y)], s1r.at[k - 1], at_y(k)) for k in (1, 3, 2)]
    for cp in c_y:
        cp.wait_recv()

    @pl.loop(0, 2 * ZL)
    def _(i):
        m, b = i // ZL, i % ZL
        total = lown[m, y, b].astype(F32) + lrecv[m, y, b].astype(F32)
        for k in range(3):
            total += s1r[k, m, b].astype(F32)
        s2f[m, b] = total
        s2[m, b] = total.astype(BF16)

    c_z = [send(ZR + k - 1, s2.at[:, lax.rem(zl + k, ZL)], s2r.at[k - 1], at_z(k)) for k in (1, 3, 2)]
    c_w += [send_w(j) for j in range(WCH - LAST_W, WCH)]
    ld_a.wait()
    ld_m.wait()
    for cp in c_z:
        cp.wait_recv()

    @pl.loop(0, 2)
    def _(m):
        total = s2f[m, zl]
        for k in range(3):
            total += s2r[k, m].astype(F32)
        anchor_now = ancv[m].astype(F32)
        pseudo = anchor_now - total / 32.0
        momentum_new = momentum_decay * momv[m] + pseudo
        momo[m] = momentum_new
        piece[m] = (anchor_now - outer_rate * (pseudo + momentum_decay * momentum_new)).astype(BF16)

    def store(i, src, dst):
        cp = pltpu.make_async_copy(src, dst, os.at[i])
        cp.start()
        return cp

    c_zg = [send(ZG + k - 1, piece, neww.at[:, y, zl, c], at_z(k)) for k in (1, 3, 2)]
    st_p = store(0, piece, neww.at[:, y, zl, c])
    st_m = store(1, momo, newm)

    ld_c.wait()
    ld_to.wait()
    for cp in c_c + c_to:
        cp.wait_recv()
    gw = SLAB // GCH

    def grad(half, j):
        return lax.dot_general(
            tbuf[half, :, pl.ds(j * gw, gw)], cbuf[...],
            (((0,), (0,)), ((), ())), preferred_element_type=F32)

    c_g = []
    for j in range(GCH):
        rows = pl.ds(j * gw, gw)
        gsend[rows] = grad(0, j).astype(BF16)
        c_g.append(send(G_ + j, gsend.at[rows], hop.at[rows], relay_to(j)))

    c_f = []

    def relay_g(j):
        rows = pl.ds(j * gw, gw)
        c_g[j].wait_recv()
        c_f.append(send(F_ + j, hop.at[rows], grecv.at[rows], relay_on(j)))

    st_p.wait()
    for cp in c_zg:
        cp.wait_recv()
    mine = neww.at[:, y, :, c]
    c_yg = [send(YG + k - 1, mine, mine, at_y(k)) for k in (1, 3, 2)]

    for cp in c_w:
        cp.wait_recv()

    @pl.loop(0, X)
    def _(k):
        rows = pl.ds(pl.multiple_of(k * TOK, TOK), TOK)
        kacc[rows] = jnp.dot(tbuf[0, rows], wbuf[0], preferred_element_type=F32)

    ld_w.wait()
    ld_tn.wait()
    for cp in c_tn:
        cp.wait_recv()
    c_k = []
    for k in (1, 3, 2, 0):
        rows = pl.ds(k * TOK, TOK)
        part = kacc[rows] + jnp.dot(tbuf[1, rows], wbuf[1], preferred_element_type=F32)
        if k:
            ksend[k - 1] = part.astype(BF16)
            c_k.append(send(K_ + k - 1, ksend.at[k - 1], krecv.at[k - 1], at_x(X - k)))
        else:
            kacc[rows] = part

    for cp in c_yg:
        cp.wait_recv()
    c_cg = send(CG, neww.at[:, :, :, c], neww.at[:, :, :, c], sibling)

    for j in range(GCH):
        gown[pl.ds(j * gw, gw)] = grad(1, j)
        if j < 2:
            relay_g(j)
    for j in range(2, GCH):
        relay_g(j)

    for cp in c_k:
        cp.wait_recv()

    @pl.loop(0, 4)
    def _(i):
        rows = pl.ds(pl.multiple_of(i * (TOK // 4), TOK // 4), TOK // 4)
        total = kacc[rows]
        for k in range(3):
            total += krecv[k, rows].astype(F32)
        kout[rows] = total.astype(BF16)

    st_k = store(2, kout, keys)
    st_g = []
    for j in range(GCH):
        c_f[j].wait_recv()
        rows = pl.ds(j * gw, gw)
        gout[rows] = (gown[rows] + grecv[rows].astype(F32)).astype(BF16)
        st_g.append(store(3 + j, gout.at[rows], wgrad.at[rows]))
    c_cg.wait_recv()
    for cp in c_l + c_w + c_c + c_to + c_tn + c_y + c_z + c_zg + c_yg + [c_cg] + c_g + c_f + c_k:
        cp.wait_send()
    for cp in [st_m, st_k] + st_g:
        cp.wait()


def emit(keys, wgrad, neww, newm, keys_o, wgrad_o, neww_o, newm_o, kv, gv, wv, mv, si, so):
    parts = [(neww.at[m, a], wv.at[m, a], neww_o.at[m, a]) for m in range(2) for a in range(Y)]
    parts += [(wgrad.at[rows], gv.at[rows], wgrad_o.at[rows])
              for rows in (pl.ds(0, SLAB // 2), pl.ds(SLAB // 2, SLAB // 2))]
    parts += [(keys, kv, keys_o), (newm, mv, newm_o)]
    loads = [pltpu.make_async_copy(a, b, si.at[i]) for i, (a, b, _) in enumerate(parts)]
    stores = [pltpu.make_async_copy(b, o, so.at[i]) for i, (_, b, o) in enumerate(parts)]
    for cp in loads:
        cp.start()
    for ld, st in zip(loads, stores):
        ld.wait()
        st.start()
    for st in stores:
        st.wait()


def shards(tokens, inner_weight, cotangent, local_weights, anchor, momentum):
    any_space = pl.BlockSpec(memory_space=pl.ANY)
    vm = pltpu.VMEM
    keys, wgrad, neww, newm = pl.pallas_call(
        kernel,
        name="diloco_step",
        out_shape=(
            jax.ShapeDtypeStruct((TOK, KW), BF16),
            jax.ShapeDtypeStruct((SLAB, KW), BF16),
            jax.ShapeDtypeStruct((2, Y, ZL, 2, ROWS, KV), BF16),
            jax.ShapeDtypeStruct((2, ROWS, KV), F32),
        ),
        in_specs=[any_space] * 6,
        out_specs=[any_space] * 4,
        scratch_shapes=[
            vm((2, X * TOK, SLAB), BF16), vm((X * TOK, KW), BF16), vm((2, SLAB, KW), BF16),
            vm((2, Y, ZL, ROWS, KV), BF16), vm((2, Y, ZL, ROWS, KV), BF16),
            vm((2, Y, ZL, ROWS, KV), BF16), vm((3, 2, ZL, ROWS, KV), BF16),
            vm((2, ZL, ROWS, KV), BF16), vm((2, ZL, ROWS, KV), F32), vm((3, 2, ROWS, KV), BF16),
            vm((2, ROWS, KV), BF16), vm((2, ROWS, KV), F32),
            vm((2, ROWS, KV), BF16), vm((2, ROWS, KV), F32),
            vm((X * TOK, KW), F32), vm((3, TOK, KW), BF16), vm((3, TOK, KW), BF16), vm((TOK, KW), BF16),
            vm((SLAB, KW), BF16), vm((SLAB, KW), BF16), vm((SLAB, KW), F32), vm((SLAB, KW), BF16),
            vm((SLAB, KW), BF16),
            pltpu.SemaphoreType.DMA((NSEM,)), pltpu.SemaphoreType.DMA((NSEM,)),
            pltpu.SemaphoreType.DMA((8,)), pltpu.SemaphoreType.DMA((3 + GCH,)),
        ],
        compiler_params=pltpu.CompilerParams(collective_id=0, has_side_effects=True),
    )(
        tokens,
        inner_weight[0],
        cotangent,
        local_weights.reshape(2, Y, ZL, 2, ROWS, KV),
        anchor.reshape(2, ROWS, KV),
        momentum.reshape(2, ROWS, KV),
    )
    kept = ((TOK, KW), BF16), ((SLAB, KW), BF16), ((2, Y, ZL, 2, ROWS, KV), BF16), ((2, ROWS, KV), F32)
    keys, wgrad, neww, newm = pl.pallas_call(
        emit,
        name="emit_outputs",
        out_shape=tuple(jax.ShapeDtypeStruct(*k) for k in kept),
        in_specs=[any_space] * 4,
        out_specs=[any_space] * 4,
        scratch_shapes=[vm(*k) for k in kept] + [pltpu.SemaphoreType.DMA((12,))] * 2,
    )(keys, wgrad, neww, newm)
    return (
        keys,
        wgrad[None],
        neww.reshape(2, Y * ZL * 2 * ROWS, KV),
        newm[:, None],
    )


def solution(mesh):
    return jax.shard_map(
        shards,
        mesh=mesh,
        in_specs=(
            P(("replica", "fsdp"), None),
            P("replica", "fsdp", None),
            P(("replica", "fsdp"), None),
            P("replica", None, "fsdp", None),
            P(None, "fsdp", "replica", None),
            P(None, "fsdp", "replica", None),
        ),
        out_specs=(
            P(("replica", "fsdp"), None),
            P("replica", "fsdp", None),
            P(None, "fsdp", None),
            P(None, "fsdp", "replica", None),
        ),
        check_vma=False,
    )
```
